32 devices in a mesh: groups: 2 (over y), dp: 4 (over z), col: 4 (over x, core).
Axes of the slice: x: 2, y: 2, z: 4, core: 2. Of those that a mesh axis runs over, the one named last changes fastest.
Arguments:
- points: float32 [16384, 256], P(('groups', 'dp')), parts along dimension 0, may hold values from -10 to 10
- point_ids: int32 [16384], P(('groups', 'dp')), parts along dimension 0, may hold values from 0 to 8191, as said below
- landmark_ids: int32 [2048], P(('groups', 'col')), parts along dimension 0, may hold values from 0 to 8191, as said below
Outputs:
- factor: float32 [2048, 1024], P('groups', 'col'), parts along dimension 0
The draws below stay inside these ranges and needn't reach their ends.
There are 2 independent parts, one for each index of `groups`. The reference program is written for one: setup_inputs(seed, part) draws one part's arguments, and reference() takes and returns one part's arrays. A program takes and returns all parts, laid end to end along the dimension named above; each array names one. Nothing has to cross between parts.
Inputs may be any that keep to these rules, and one draw needn't show every extreme that they name: `point_ids`: a permutation of the numbers 0 to 8191. `landmark_ids`: 1024 distinct ids, each the id of some point; the indices of dp that hold these points hold unequal numbers of them.
All inputs are finite; a program needn't handle non-finite values.
Results may differ from the reference program's by a relative error of at most 0.0003.
Values sent between devices are 32-bit elements; how exact they have to be, the bound alone decides.
No kernel may reach another device: no remote copies, remote signals or barrier semaphores. Data moves between devices by JAX's collectives and lax.ppermute only.
A program may use at most 64 MiB of HBM per device.

```python
import math
import jax
import jax.numpy as jnp
from jax import lax

DIM = 256
LAND = 1024
ROWS_DEV = 2048
NPTS = 8192


def landmark_choice(key):
    base = jax.random.fold_in(key, 7)
    order = jax.random.permutation(jax.random.fold_in(base, 1), NPTS).astype(jnp.int32)
    owners = NPTS // ROWS_DEV
    levels = jax.random.randint(jax.random.fold_in(base, 2), (owners,), 0, 4)
    owner_of = jnp.arange(NPTS, dtype=jnp.int32) // ROWS_DEV
    score = jax.random.randint(jax.random.fold_in(base, 3), (NPTS,), 0, 2048) + levels[owner_of] * 512
    composite = score * NPTS + jnp.arange(NPTS, dtype=jnp.int32)
    values, picked = lax.top_k(composite, LAND)
    return (order, order[picked])


def draw_point_ids(key, part):
    order, chosen = landmark_choice(key)
    return order


def draw_landmark_ids(key, part):
    order, chosen = landmark_choice(key)
    return chosen


def log_spread(key, shape, low, high):
    unit = jax.random.uniform(key, shape, jnp.float32)
    return jnp.exp(math.log(low) + unit * (math.log(high) - math.log(low)))


def draw_points(key, part):
    base = jax.random.fold_in(key, 11)
    cluster_count = max(NPTS // 256, 2)
    member = jax.random.randint(jax.random.fold_in(base, 1), (NPTS,), 0, cluster_count)
    point_spread = log_spread(jax.random.fold_in(base, 2), (NPTS,), 0.6, 1.4)
    means = 1.2 * jax.random.truncated_normal(jax.random.fold_in(base, 3), -4.0, 4.0, (cluster_count, DIM), jnp.float32)
    cluster_spread = log_spread(jax.random.fold_in(base, 4), (cluster_count,), 0.45, 0.8)
    noise = jax.random.truncated_normal(jax.random.fold_in(base, 5), -4.0, 4.0, (NPTS, DIM), jnp.float32)
    spread = cluster_spread[member] * point_spread
    return means[member] + spread[:, None] * noise


def setup_inputs(seed: int = 0, part: int = 0) -> dict:
    seeds = jax.random.split(jax.random.key(seed), 4)
    part_splits = jax.random.split(jax.random.fold_in(seeds[3], part), 4)
    return {
        "points": draw_points(jax.random.fold_in(jax.random.fold_in(seeds[3], part), 71), part),
        "point_ids": draw_point_ids(jax.random.fold_in(jax.random.fold_in(seeds[3], part), 71), part),
        "landmark_ids": draw_landmark_ids(jax.random.fold_in(jax.random.fold_in(seeds[3], part), 71), part),
    }


precise = lax.Precision.HIGHEST

def kernel_panel(points, centers):
    point_norms = jnp.sum(points * points, axis=1)
    center_norms = jnp.sum(centers * centers, axis=1)
    inner = lax.dot_general(points.astype(jnp.float32), centers.astype(jnp.float32), (((1,), (1,)), ((), ())), precision=precise, preferred_element_type=jnp.float32)
    distance = point_norms[:, None] + center_norms[None, :] - 2.0 * inner
    return jnp.exp(distance * (-2.0 / points.shape[1]))

def reference(points, point_ids, landmark_ids):
    count = point_ids.shape[0]
    positions = jnp.zeros((count,), jnp.int32).at[point_ids.astype(jnp.int32)].set(jnp.arange(count, dtype=jnp.int32))
    centers = points[positions[landmark_ids.astype(jnp.int32)]]
    panel = kernel_panel(points, centers)
    gram = lax.dot_general(panel.astype(jnp.float32), panel.astype(jnp.float32), (((0,), (0,)), ((), ())), precision=precise, preferred_element_type=jnp.float32)
    lower_factor = jnp.linalg.cholesky(gram)
    return lower_factor.T
```

```python
import functools

import jax
import jax.numpy as jnp
from jax import lax
from jax.experimental import pallas as pl
from jax.experimental.pallas import tpu as pltpu
from jax.sharding import PartitionSpec as P

LAND = 1024
NB = 128
PAIR = 2 * NB
STRIPS = NB // 8
BLOCKS = LAND // NB

F32 = jnp.float32
BF16 = jnp.bfloat16
precise = lax.Precision.HIGHEST


def nt(a, b):
    return lax.dot_general(a, b, (((1,), (1,)), ((), ())), precision=precise, preferred_element_type=F32)


def nt16(a, b):
    return lax.dot_general(a, b, (((1,), (1,)), ((), ())), preferred_element_type=F32)


def split3(x):
    high = x.astype(BF16)
    rest = x - high.astype(F32)
    mid = rest.astype(BF16)
    low = (rest - mid.astype(F32)).astype(BF16)
    return high, mid, low


def log2(n):
    bits = n.bit_length() - 1
    assert n == 1 << bits
    return bits


def mirror(k):
    return (2 << k) - 1


def gray(i):
    return i ^ (i >> 1)


def ungray(g, bits):
    i = g
    for s in range(1, bits):
        i = i ^ (g >> s)
    return i


def swap(x, axis, mask):
    n = lax.axis_size(axis)
    return lax.ppermute(x, axis, [(i, i ^ mask) for i in range(n)])


def column_groups(nx):
    if nx == 4:
        return [[(0,), (7,)], [(1,), (6,)], [(2,), (5,)], [(3,), (4,)]]
    assert nx == 2
    return [[(0, 1), (6, 7)], [(2, 3), (4, 5)]]


def group_blocks(group):
    return [(j, c) for cols in group for c in cols for j in range(c, BLOCKS)]


class Plan:
    def __init__(self, dp, col):
        self.dp, self.col = dp, col
        self.nx = col // 2
        self.xbits, self.zbits = log2(self.nx), log2(dp)
        self.groups = column_groups(self.nx)
        self.rows = len(group_blocks(self.groups[0])) * NB
        rows = self.rows // 2
        self.halved = 0
        while self.halved < self.zbits and rows % 16 == 0:
            rows //= 2
            self.halved += 1
        self.piece = rows
        self.pieces = 2 << self.halved

    def own_piece(self, col_index, dp_index):
        g = gray(dp_index)
        s = col_index & 1
        for k in range(self.halved):
            s = (s << 1) | ((g >> k) & 1)
        return s


def pick_kernel(lid_ref, pid_ref, points_ref, out_ref):
    matches = jnp.where(lid_ref[...] == pid_ref[...], 1.0, 0.0).astype(BF16)
    high, mid, low = split3(points_ref[...])
    dot = functools.partial(jnp.dot, preferred_element_type=F32)
    out_ref[...] = (dot(matches, high) + dot(matches, mid)) + dot(matches, low)


def pick(landmark_ids, point_ids, points):
    n = landmark_ids.shape[0]
    return pl.pallas_call(
        pick_kernel,
        out_shape=jax.ShapeDtypeStruct((n, points.shape[1]), F32),
        name="pick",
    )(landmark_ids.reshape(n, 1), point_ids.reshape(1, -1), points)


def gram_kernel(plan, where_ref, points_ref, centers_ref, out_ref, centers, panel, tall):
    col, me = where_ref[0], where_ref[1]
    land_cols = LAND // plan.col
    half, dim = points_ref.shape
    for r in range(plan.col):
        rx, rc = r & (plan.nx - 1), r >> plan.xbits
        x = ungray(gray(col >> 1) ^ rx, plan.xbits)
        owner = (x << 1) | ((col & 1) ^ rc)
        at = pl.multiple_of(owner * land_cols, land_cols)
        centers[pl.ds(at, land_cols), :] = centers_ref[r * land_cols : (r + 1) * land_cols, :]
    pts = points_ref[...]
    point_norms = nt(jnp.ones((8, dim), F32), pts * pts)[0:1, :]
    for b in range(LAND // PAIR):
        c = centers[b * PAIR : (b + 1) * PAIR, :]
        center_norms = jnp.sum(c * c, axis=1, keepdims=True)
        distance = point_norms + center_norms - 2.0 * nt(c, pts)
        panel[b * PAIR : (b + 1) * PAIR, :] = jnp.exp(distance * (-2.0 / dim))
    for x, group in enumerate(plan.groups):

        @pl.when((col >> 1) == x)
        def _():
            at = 0
            for cols in group:
                lo = cols[0] * NB
                product = nt(panel[lo:, :], panel[lo : lo + len(cols) * NB, :])
                for k, c in enumerate(cols):
                    rows = LAND - c * NB
                    tall[at : at + rows, :] = product[k * NB :, k * NB : (k + 1) * NB]
                    at += rows

    for r in range(plan.pieces):
        start = pl.multiple_of((me ^ r) * plan.piece, 8)
        out_ref[r * plan.piece : (r + 1) * plan.piece, :] = tall[pl.ds(start, plan.piece), :]


def gram_pieces(plan, where, points, centers):
    half = points.shape[0] // 2
    dim = points.shape[1]
    return pl.pallas_call(
        functools.partial(gram_kernel, plan),
        grid_spec=pltpu.PrefetchScalarGridSpec(
            num_scalar_prefetch=1,
            grid=(1,),
            in_specs=[
                pl.BlockSpec((half, dim), lambda i, where: (where[0] & 1, 0)),
                pl.BlockSpec((LAND, dim), lambda i, where: (0, 0)),
            ],
            out_specs=pl.BlockSpec((plan.rows, NB), lambda i, where: (0, 0)),
            scratch_shapes=[
                pltpu.VMEM((LAND, dim), F32),
                pltpu.VMEM((LAND, half), F32),
                pltpu.VMEM((plan.rows, NB), F32),
            ],
        ),
        out_shape=jax.ShapeDtypeStruct((plan.rows, NB), F32),
        name="gram",
    )(where, points, centers)


def lanecast(x, lane):
    index = jnp.full((8, NB), lane, jnp.int32)
    return jnp.take_along_axis(x, index, axis=1, mode="promise_in_bounds")


def rowcast(x, row):
    return jnp.broadcast_to(x[row : row + 1, :], (8, NB))


def eliminate(rows, s, lane, sub):
    own, lo = rows[s], 8 * s
    columns = [lanecast(own, lo + j) for j in range(8)]
    p = {(i, j): rowcast(columns[j], i) for j in range(8) for i in range(j + 1)}
    inside = (lane >= lo) & (lane < lo + 8)
    t = [jnp.where(inside, jnp.where(lane == lo + j, 1.0, 0.0), rowcast(own, j)) for j in range(8)]
    inverse = []
    for j in range(8):
        inverse.append(1.0 / p[j, j])
        for i in range(j + 1, 8):
            m = p[j, i] * inverse[j]
            for l in range(i, 8):
                p[i, l] = p[i, l] - m * p[j, l]
            t[i] = t[i] - m * t[j]
    scaled = t[0] * lax.rsqrt(p[0, 0])
    for j in range(1, 8):
        scaled = jnp.where(sub == j, t[j] * lax.rsqrt(p[j, j]), scaled)
    if s + 1 < STRIPS:
        v = [t[j] * inverse[j] for j in range(8)]
        for j in range(7, -1, -1):
            for i in range(j):
                v[i] = v[i] - (p[i, j] * inverse[i]) * v[j]
        for q in range(s + 1, STRIPS):
            columns = [lanecast(rows[q], lo + j) for j in range(8)]
            rest = jnp.where(inside, 0.0, rows[q])
            for j in range(7, -1, -1):
                rest = rest - columns[j] * v[j]
            rows[q] = rest
    return scaled


def factor_inverse(block, inverse):
    lane = lax.broadcasted_iota(jnp.int32, (8, NB), 1)
    sub = lax.broadcasted_iota(jnp.int32, (8, NB), 0)
    rows = [block[8 * q : 8 * q + 8, :] for q in range(STRIPS)]
    for s in range(STRIPS):
        scaled = eliminate(rows, s, lane, sub)
        inverse[8 * s : 8 * s + 8, :] = jnp.where(lane < 8 * (s + 1), scaled, 0.0)


def cholesky_kernel(plan, where_ref, pieces_ref, out_ref, tall, a, block, inv1, inv2, l21):
    col, me = where_ref[0], where_ref[1]
    zmask = (1 << plan.halved) - 1
    for r in range(plan.pieces * plan.nx):
        rz = r & zmask
        rx = (r >> plan.halved) & (plan.nx - 1)
        rc = r >> (plan.halved + plan.xbits)
        x = ungray(gray(col >> 1) ^ rx, plan.xbits)
        piece = me ^ ((rc << plan.halved) | rz)
        start = pl.multiple_of(x * plan.rows + piece * plan.piece, 8)
        tall[pl.ds(start, plan.piece), :] = pieces_ref[r * plan.piece : (r + 1) * plan.piece, :]
    at = 0
    for group in plan.groups:
        for j, c in group_blocks(group):
            a[j * NB : (j + 1) * NB, c * NB : (c + 1) * NB] = tall[at : at + NB, :]
            at += NB

    row = lax.broadcasted_iota(jnp.int32, (NB, NB), 0)
    column = lax.broadcasted_iota(jnp.int32, (NB, NB), 1)

    def step(k, carry):
        base = pl.multiple_of((k // 2) * PAIR, PAIR)
        first = (k % 2) == 0
        for t in range(LAND // PAIR):
            lo = t * PAIR

            @pl.when(k == 2 * t)
            def _():
                if t:
                    update = nt(a[lo:, :lo], a[lo : lo + PAIR, :lo])
                    a[lo:, lo : lo + PAIR] = a[lo:, lo : lo + PAIR] - update
                block[...] = a[lo : lo + NB, lo : lo + NB]

        @pl.when(jnp.logical_not(first))
        def _():
            below = nt(a[pl.ds(base + NB, NB), pl.ds(base, NB)], inv2[...])
            l21[...] = below
            inv1[...] = inv2[...]
            block[...] = a[pl.ds(base + NB, NB), pl.ds(base + NB, NB)] - nt(below, below)

        factor_inverse(block, inv2)

        for t in range(LAND // PAIR):
            lo = t * PAIR

            @pl.when(k == 2 * t + 1)
            def _():
                left = nt(a[lo:, lo : lo + NB], inv1[...])
                right = a[lo + NB :, lo + NB : lo + PAIR] - nt(left[NB:, :], l21[...])
                right = nt(right, inv2[...])
                a[lo : lo + NB, lo : lo + NB] = jnp.where(column <= row, left[:NB, :], 0.0)
                a[lo + NB :, lo : lo + NB] = left[NB:, :]
                a[lo + NB : lo + PAIR, lo + NB : lo + PAIR] = jnp.where(column <= row, right[:NB, :], 0.0)
                if lo + PAIR < LAND:
                    a[lo + PAIR :, lo + NB : lo + PAIR] = right[NB:, :]

        return carry

    lax.fori_loop(0, BLOCKS, step, 0)

    width = LAND // plan.col
    out_ref[...] = jnp.zeros(out_ref.shape, F32)
    for c in range(plan.col):

        @pl.when(col == c)
        def _():
            for j in range(width // NB):
                at = c * width + j * NB
                for i in range(at // NB + 1):
                    out_ref[i * NB : (i + 1) * NB, j * NB : (j + 1) * NB] = a[at : at + NB, i * NB : (i + 1) * NB].T


def factor(plan, where, pieces):
    total = plan.rows * plan.nx
    width = LAND // plan.col
    return pl.pallas_call(
        functools.partial(cholesky_kernel, plan),
        grid_spec=pltpu.PrefetchScalarGridSpec(
            num_scalar_prefetch=1,
            grid=(1,),
            in_specs=[pl.BlockSpec((total, NB), lambda i, where: (0, 0))],
            out_specs=pl.BlockSpec((LAND, width), lambda i, where: (0, 0)),
            scratch_shapes=[
                pltpu.VMEM((total, NB), F32),
                pltpu.VMEM((LAND, LAND), F32),
                pltpu.VMEM((NB, NB), F32),
                pltpu.VMEM((NB, NB), F32),
                pltpu.VMEM((NB, NB), F32),
                pltpu.VMEM((NB, NB), F32),
            ],
        ),
        out_shape=jax.ShapeDtypeStruct((LAND, width), F32),
        name="factor",
    )(where, pieces)


def local(points, point_ids, landmark_ids):
    plan = Plan(lax.axis_size("dp"), lax.axis_size("col"))
    col_index, dp_index = lax.axis_index("col"), lax.axis_index("dp")
    where = jnp.stack([col_index, plan.own_piece(col_index, dp_index)]).astype(jnp.int32)

    centers = pick(landmark_ids, point_ids, points)
    for k in range(plan.zbits):
        centers = centers + swap(centers, "dp", mirror(k))
    for k in range(plan.xbits):
        centers = jnp.concatenate([centers, swap(centers, "col", 2 * mirror(k))])
    centers = jnp.concatenate([centers, swap(centers, "col", 1)])

    held = gram_pieces(plan, where, points, centers)
    half = plan.rows // 2
    held = held[:half] + swap(held[half:], "col", 1)
    for k in range(plan.halved):
        half = half // 2
        held = held[:half] + swap(held[half:], "dp", mirror(k))
    for k in range(plan.halved, plan.zbits):
        held = held + swap(held, "dp", mirror(k))
    for k in reversed(range(plan.halved)):
        held = jnp.concatenate([held, swap(held, "dp", mirror(k))])
    for k in range(plan.xbits):
        held = jnp.concatenate([held, swap(held, "col", 2 * mirror(k))])
    held = jnp.concatenate([held, swap(held, "col", 1)])
    return factor(plan, where, held)


def solution(mesh):
    in_specs = (P(("groups", "dp"), None), P(("groups", "dp")), P(("groups", "col")))
    out_specs = P("groups", "col")
    return jax.shard_map(local, mesh=mesh, in_specs=in_specs, out_specs=out_specs, check_vma=False)
```

```python
import functools

import jax
import jax.numpy as jnp
from jax import lax
from jax.experimental import pallas as pl
from jax.experimental.pallas import tpu as pltpu
from jax.sharding import PartitionSpec as P

LAND = 1024
NB = 128
PAIR = 2 * NB
STRIPS = NB // 8
BLOCKS = LAND // NB

F32 = jnp.float32
BF16 = jnp.bfloat16
precise = lax.Precision.HIGHEST


def nt(a, b):
    return lax.dot_general(a, b, (((1,), (1,)), ((), ())), precision=precise, preferred_element_type=F32)


def nt16(a, b):
    return lax.dot_general(a, b, (((1,), (1,)), ((), ())), preferred_element_type=F32)


def split2(x):
    high = x.astype(BF16)
    return high, (x - high.astype(F32)).astype(BF16)


def split3(x):
    high = x.astype(BF16)
    rest = x - high.astype(F32)
    mid = rest.astype(BF16)
    low = (rest - mid.astype(F32)).astype(BF16)
    return high, mid, low


def log2(n):
    bits = n.bit_length() - 1
    assert n == 1 << bits
    return bits


def mirror(k):
    return (2 << k) - 1


def gray(i):
    return i ^ (i >> 1)


def ungray(g, bits):
    i = g
    for s in range(1, bits):
        i = i ^ (g >> s)
    return i


def swap(x, axis, mask):
    n = lax.axis_size(axis)
    return lax.ppermute(x, axis, [(i, i ^ mask) for i in range(n)])


def column_groups(nx):
    if nx == 4:
        return [[(0,), (7,)], [(1,), (6,)], [(2,), (5,)], [(3,), (4,)]]
    assert nx == 2
    return [[(0, 1), (6, 7)], [(2, 3), (4, 5)]]


def group_blocks(group):
    return [(j, c) for cols in group for c in cols for j in range(c, BLOCKS)]


class Plan:
    def __init__(self, dp, col):
        self.dp, self.col = dp, col
        self.nx = col // 2
        self.xbits, self.zbits = log2(self.nx), log2(dp)
        self.groups = column_groups(self.nx)
        self.rows = len(group_blocks(self.groups[0])) * NB
        rows = self.rows // 2
        self.halved = 0
        while self.halved < self.zbits and rows % 16 == 0:
            rows //= 2
            self.halved += 1
        self.piece = rows
        self.pieces = 2 << self.halved

    def own_piece(self, col_index, dp_index):
        g = gray(dp_index)
        s = col_index & 1
        for k in range(self.halved):
            s = (s << 1) | ((g >> k) & 1)
        return s


def pick_kernel(lid_ref, pid_ref, points_ref, out_ref):
    matches = jnp.where(lid_ref[...] == pid_ref[...], 1.0, 0.0).astype(BF16)
    high, mid, low = split3(points_ref[...])
    dot = functools.partial(jnp.dot, preferred_element_type=F32)
    out_ref[...] = (dot(matches, high) + dot(matches, mid)) + dot(matches, low)


def pick(landmark_ids, point_ids, points):
    n = landmark_ids.shape[0]
    return pl.pallas_call(
        pick_kernel,
        out_shape=jax.ShapeDtypeStruct((n, points.shape[1]), F32),
        out_specs=pl.BlockSpec(memory_space=pltpu.VMEM),
        compiler_params=pltpu.CompilerParams(vmem_limit_bytes=36 << 20),
        name="pick",
    )(landmark_ids.reshape(n, 1), point_ids.reshape(1, -1), points)


def gram_kernel(plan, where_ref, points_ref, centers_ref, kept_ref, sent_ref, centers, panel_high, panel_mid, tall):
    col, me = where_ref[0], where_ref[1]
    land_cols = LAND // plan.col
    half, dim = points_ref.shape
    for r in range(plan.col):
        rx, rc = r & (plan.nx - 1), r >> plan.xbits
        x = ungray(gray(col >> 1) ^ rx, plan.xbits)
        owner = (x << 1) | ((col & 1) ^ rc)
        at = pl.multiple_of(owner * land_cols, land_cols)
        centers[pl.ds(at, land_cols), :] = centers_ref[r * land_cols : (r + 1) * land_cols, :]
    pts = points_ref[...]
    point_norms = nt(jnp.ones((8, dim), F32), pts * pts)[0:1, :]
    high, mid, low = split3(pts)
    right = jnp.concatenate([low, mid, high, mid, high, high], axis=1)
    for b in range(LAND // PAIR):
        block = slice(b * PAIR, (b + 1) * PAIR)
        c = centers[block, :]
        center_norms = jnp.sum(c * c, axis=1, keepdims=True)
        high, mid, low = split3(c)
        inner = nt16(jnp.concatenate([high, mid, low, high, mid, high], axis=1), right)
        distance = point_norms + center_norms - 2.0 * inner
        values = jnp.exp(distance * (-2.0 / dim))
        panel_high[block, :], panel_mid[block, :] = split2(values)
    for x, group in enumerate(plan.groups):

        @pl.when((col >> 1) == x)
        def _():
            at = 0
            for cols in group:
                lo = cols[0] * NB
                some = slice(lo, lo + len(cols) * NB)
                product = nt16(
                    jnp.concatenate([panel_high[lo:, :], panel_mid[lo:, :], panel_high[lo:, :]], axis=1),
                    jnp.concatenate([panel_mid[some, :], panel_high[some, :], panel_high[some, :]], axis=1),
                )
                for k, c in enumerate(cols):
                    rows = LAND - c * NB
                    tall[at : at + rows, :] = product[k * NB :, k * NB : (k + 1) * NB]
                    at += rows

    for r in range(plan.pieces):
        start = pl.multiple_of((me ^ r) * plan.piece, 8)
        out, q = (kept_ref, r) if r < plan.pieces // 2 else (sent_ref, r - plan.pieces // 2)
        out[q * plan.piece : (q + 1) * plan.piece, :] = tall[pl.ds(start, plan.piece), :]


def gram_pieces(plan, where, points, centers):
    half = points.shape[0] // 2
    dim = points.shape[1]
    return pl.pallas_call(
        functools.partial(gram_kernel, plan),
        grid_spec=pltpu.PrefetchScalarGridSpec(
            num_scalar_prefetch=1,
            grid=(1,),
            in_specs=[
                pl.BlockSpec((half, dim), lambda i, where: (where[0] & 1, 0)),
                pl.BlockSpec(memory_space=pltpu.VMEM),
            ],
            out_specs=[pl.BlockSpec(memory_space=pltpu.VMEM)] * 2,
            scratch_shapes=[
                pltpu.VMEM((LAND, dim), F32),
                pltpu.VMEM((LAND, half), BF16),
                pltpu.VMEM((LAND, half), BF16),
                pltpu.VMEM((plan.rows, NB), F32),
            ],
        ),
        out_shape=[jax.ShapeDtypeStruct((plan.rows // 2, NB), F32)] * 2,
        compiler_params=pltpu.CompilerParams(vmem_limit_bytes=36 << 20),
        name="gram",
    )(where, points, centers)


def lanecast(x, lane):
    index = jnp.full((8, NB), lane, jnp.int32)
    return jnp.take_along_axis(x, index, axis=1, mode="promise_in_bounds")


def rowcast(x, row):
    return jnp.broadcast_to(x[row : row + 1, :], (8, NB))


def eliminate(rows, s, lane, sub):
    own, lo = rows[s], 8 * s
    columns = [lanecast(own, lo + j) for j in range(8)]
    p = {(i, j): rowcast(columns[j], i) for j in range(8) for i in range(j + 1)}
    inside = (lane >= lo) & (lane < lo + 8)
    t = [jnp.where(inside, jnp.where(lane == lo + j, 1.0, 0.0), rowcast(own, j)) for j in range(8)]
    inverse = []
    for j in range(8):
        inverse.append(1.0 / p[j, j])
        for i in range(j + 1, 8):
            m = p[j, i] * inverse[j]
            for l in range(i, 8):
                p[i, l] = p[i, l] - m * p[j, l]
            t[i] = t[i] - m * t[j]
    scaled = t[0] * lax.rsqrt(p[0, 0])
    for j in range(1, 8):
        scaled = jnp.where(sub == j, t[j] * lax.rsqrt(p[j, j]), scaled)
    if s + 1 < STRIPS:
        v = [t[j] * inverse[j] for j in range(8)]
        for j in range(7, -1, -1):
            for i in range(j):
                v[i] = v[i] - (p[i, j] * inverse[i]) * v[j]
        for q in range(s + 1, STRIPS):
            columns = [lanecast(rows[q], lo + j) for j in range(8)]
            rest = jnp.where(inside, 0.0, rows[q])
            for j in range(7, -1, -1):
                rest = rest - columns[j] * v[j]
            rows[q] = rest
    return scaled


def factor_inverse(block, inverse):
    lane = lax.broadcasted_iota(jnp.int32, (8, NB), 1)
    sub = lax.broadcasted_iota(jnp.int32, (8, NB), 0)
    rows = [block[8 * q : 8 * q + 8, :] for q in range(STRIPS)]
    for s in range(STRIPS):
        scaled = eliminate(rows, s, lane, sub)
        inverse[8 * s : 8 * s + 8, :] = jnp.where(lane < 8 * (s + 1), scaled, 0.0)


def cholesky_kernel(plan, where_ref, here0, here1, there0, there1, out_ref, tall, a, block, inv1, inv2, l21):
    col, me = where_ref[0], where_ref[1]
    low = plan.halved - 1
    for rc, rz, pieces_ref in ((0, 0, here0), (0, 1, here1), (1, 0, there0), (1, 1, there1)):
        for r in range(plan.nx << low):
            x = ungray(gray(col >> 1) ^ (r >> low), plan.xbits)
            piece = me ^ ((rc << plan.halved) | (rz << low) | (r & ((1 << low) - 1)))
            start = pl.multiple_of(x * plan.rows + piece * plan.piece, 8)
            tall[pl.ds(start, plan.piece), :] = pieces_ref[r * plan.piece : (r + 1) * plan.piece, :]
    at = 0
    for group in plan.groups:
        for j, c in group_blocks(group):
            a[j * NB : (j + 1) * NB, c * NB : (c + 1) * NB] = tall[at : at + NB, :]
            at += NB

    row = lax.broadcasted_iota(jnp.int32, (NB, NB), 0)
    column = lax.broadcasted_iota(jnp.int32, (NB, NB), 1)

    def step(k, carry):
        base = pl.multiple_of((k // 2) * PAIR, PAIR)
        first = (k % 2) == 0
        for t in range(LAND // PAIR):
            lo = t * PAIR

            @pl.when(k == 2 * t)
            def _():
                if t:
                    update = nt(a[lo:, :lo], a[lo : lo + PAIR, :lo])
                    a[lo:, lo : lo + PAIR] = a[lo:, lo : lo + PAIR] - update
                block[...] = a[lo : lo + NB, lo : lo + NB]

        @pl.when(jnp.logical_not(first))
        def _():
            below = nt(a[pl.ds(base + NB, NB), pl.ds(base, NB)], inv2[...])
            l21[...] = below
            inv1[...] = inv2[...]
            block[...] = a[pl.ds(base + NB, NB), pl.ds(base + NB, NB)] - nt(below, below)

        factor_inverse(block, inv2)

        for t in range(LAND // PAIR):
            lo = t * PAIR

            @pl.when(k == 2 * t + 1)
            def _():
                left = nt(a[lo:, lo : lo + NB], inv1[...])
                right = a[lo + NB :, lo + NB : lo + PAIR] - nt(left[NB:, :], l21[...])
                right = nt(right, inv2[...])
                a[lo : lo + NB, lo : lo + NB] = jnp.where(column <= row, left[:NB, :], 0.0)
                a[lo + NB :, lo : lo + NB] = left[NB:, :]
                a[lo + NB : lo + PAIR, lo + NB : lo + PAIR] = jnp.where(column <= row, right[:NB, :], 0.0)
                if lo + PAIR < LAND:
                    a[lo + PAIR :, lo + NB : lo + PAIR] = right[NB:, :]

        return carry

    lax.fori_loop(0, BLOCKS, step, 0)

    width = LAND // plan.col
    out_ref[...] = jnp.zeros(out_ref.shape, F32)
    for c in range(plan.col):

        @pl.when(col == c)
        def _():
            for j in range(width // NB):
                at = c * width + j * NB
                for i in range(at // NB + 1):
                    out_ref[i * NB : (i + 1) * NB, j * NB : (j + 1) * NB] = a[at : at + NB, i * NB : (i + 1) * NB].T


def factor(plan, where, parts):
    total = plan.rows * plan.nx
    width = LAND // plan.col
    return pl.pallas_call(
        functools.partial(cholesky_kernel, plan),
        grid_spec=pltpu.PrefetchScalarGridSpec(
            num_scalar_prefetch=1,
            grid=(1,),
            in_specs=[pl.BlockSpec(memory_space=pltpu.VMEM)] * 4,
            out_specs=pl.BlockSpec((LAND, width), lambda i, where: (0, 0)),
            scratch_shapes=[
                pltpu.VMEM((total, NB), F32),
                pltpu.VMEM((LAND, LAND), F32),
                pltpu.VMEM((NB, NB), F32),
                pltpu.VMEM((NB, NB), F32),
                pltpu.VMEM((NB, NB), F32),
                pltpu.VMEM((NB, NB), F32),
            ],
        ),
        out_shape=jax.ShapeDtypeStruct((LAND, width), F32),
        compiler_params=pltpu.CompilerParams(vmem_limit_bytes=28 << 20),
        name="factor",
    )(where, *parts)


def local(points, point_ids, landmark_ids):
    plan = Plan(lax.axis_size("dp"), lax.axis_size("col"))
    col_index, dp_index = lax.axis_index("col"), lax.axis_index("dp")
    where = jnp.stack([col_index, plan.own_piece(col_index, dp_index)]).astype(jnp.int32)

    centers = pick(landmark_ids, point_ids, points)
    first, second = jnp.split(centers, 2)
    steps = list(range(plan.zbits))
    for k, other in zip(steps, [1, 0] + steps[2:]):
        first = first + swap(first, "dp", mirror(k))
        second = second + swap(second, "dp", mirror(other))
    centers = over_x(plan, jnp.concatenate([first, second]))
    centers = jnp.concatenate([centers, swap(centers, "col", 1)])

    kept, sent = gram_pieces(plan, where, points, centers)
    held = kept + swap(sent, "col", 1)
    for k in range(plan.halved):
        half = held.shape[0] // 2
        held = held[:half] + swap(held[half:], "dp", mirror(k))
    for k in range(plan.halved, plan.zbits):
        held = held + swap(held, "dp", mirror(k))
    for k in reversed(range(1, plan.halved)):
        held = jnp.concatenate([held, swap(held, "dp", mirror(k))])
    beside = swap(held, "dp", mirror(0))
    here = [over_x(plan, held), over_x(plan, beside)]
    there = [swap(part, "col", 1) for part in here]
    return factor(plan, where, here + there)


def over_x(plan, part):
    for k in range(plan.xbits):
        part = jnp.concatenate([part, swap(part, "col", 2 * mirror(k))])
    return part


def solution(mesh):
    in_specs = (P(("groups", "dp"), None), P(("groups", "dp")), P(("groups", "col")))
    out_specs = P("groups", "col")
    return jax.shard_map(local, mesh=mesh, in_specs=in_specs, out_specs=out_specs, check_vma=False)
```

```python
import functools

import jax
import jax.numpy as jnp
from jax import lax
from jax.experimental import pallas as pl
from jax.experimental.pallas import tpu as pltpu
from jax.sharding import PartitionSpec as P

LAND = 1024
NB = 128
PAIR = 2 * NB
STRIPS = NB // 8
BLOCKS = LAND // NB

F32 = jnp.float32
BF16 = jnp.bfloat16
precise = lax.Precision.HIGHEST


def nt(a, b):
    return lax.dot_general(a, b, (((1,), (1,)), ((), ())), precision=precise, preferred_element_type=F32)


def nt16(a, b):
    return lax.dot_general(a, b, (((1,), (1,)), ((), ())), preferred_element_type=F32)


def six(x, other):
    high, mid, low = split3(x)
    return jnp.concatenate([low, mid, high, mid, high, high] if other else [high, mid, low, high, mid, high], axis=1)


def nt6(a, b):
    return nt16(six(a, False), six(b, True))


def split2(x):
    high = x.astype(BF16)
    return high, (x - high.astype(F32)).astype(BF16)


def split3(x):
    high = x.astype(BF16)
    rest = x - high.astype(F32)
    mid = rest.astype(BF16)
    low = (rest - mid.astype(F32)).astype(BF16)
    return high, mid, low


def log2(n):
    bits = n.bit_length() - 1
    assert n == 1 << bits
    return bits


def mirror(k):
    return (2 << k) - 1


def gray(i):
    return i ^ (i >> 1)


def ungray(g, bits):
    i = g
    for s in range(1, bits):
        i = i ^ (g >> s)
    return i


def swap(x, axis, mask):
    n = lax.axis_size(axis)
    return lax.ppermute(x, axis, [(i, i ^ mask) for i in range(n)])


def column_groups(nx):
    if nx == 4:
        return [[(0,), (7,)], [(1,), (6,)], [(2,), (5,)], [(3,), (4,)]]
    assert nx == 2
    return [[(0, 1), (6, 7)], [(2, 3), (4, 5)]]


def group_blocks(group):
    return [(j, c) for cols in group for c in cols for j in range(c, BLOCKS)]


class Plan:
    def __init__(self, dp, col):
        self.dp, self.col = dp, col
        self.nx = col // 2
        self.xbits, self.zbits = log2(self.nx), log2(dp)
        self.groups = column_groups(self.nx)
        self.rows = len(group_blocks(self.groups[0])) * NB
        rows = self.rows // 2
        self.halved = 0
        while self.halved < max(1, self.zbits - 1) and rows % 16 == 0:
            rows //= 2
            self.halved += 1
        self.piece = rows
        self.pieces = 2 << self.halved

    def own_piece(self, col_index, dp_index):
        g = gray(dp_index)
        s = col_index & 1
        for k in range(self.halved):
            s = (s << 1) | ((g >> k) & 1)
        return s


def pick_kernel(lid_ref, pid_ref, points_ref, out_ref):
    matches = jnp.where(lid_ref[...] == pid_ref[...], 1.0, 0.0).astype(BF16)
    high, mid, low = split3(points_ref[...])
    dot = functools.partial(jnp.dot, preferred_element_type=F32)
    out_ref[...] = (dot(matches, high) + dot(matches, mid)) + dot(matches, low)


def pick(landmark_ids, point_ids, points):
    n = landmark_ids.shape[0]
    return pl.pallas_call(
        pick_kernel,
        out_shape=jax.ShapeDtypeStruct((n, points.shape[1]), F32),
        out_specs=pl.BlockSpec(memory_space=pltpu.VMEM),
        compiler_params=pltpu.CompilerParams(vmem_limit_bytes=36 << 20),
        name="pick",
    )(landmark_ids.reshape(n, 1), point_ids.reshape(1, -1), points)


def gram_kernel(
    plan, where_ref, points_ref, here0, here1, there0, there1, kept_ref, sent_ref, centers, panel_high, panel_mid, tall
):
    col, me = where_ref[0], where_ref[1]
    some = LAND // plan.col // 2
    half, dim = points_ref.shape
    for part, centers_ref in enumerate((here0, here1, there0, there1)):
        for rx in range(plan.nx):
            x = ungray(gray(col >> 1) ^ rx, plan.xbits)
            owner = (x << 1) | ((col & 1) ^ (part // 2))
            at = pl.multiple_of((2 * owner + part % 2) * some, some)
            centers[pl.ds(at, some), :] = centers_ref[rx * some : (rx + 1) * some, :]
    pts = points_ref[...]
    point_norms = nt(jnp.ones((8, dim), F32), pts * pts)[0:1, :]
    right = six(pts, True)
    for b in range(LAND // PAIR):
        block = slice(b * PAIR, (b + 1) * PAIR)
        c = centers[block, :]
        center_norms = jnp.sum(c * c, axis=1, keepdims=True)
        inner = nt16(six(c, False), right)
        distance = point_norms + center_norms - 2.0 * inner
        values = jnp.exp(distance * (-2.0 / dim))
        panel_high[block, :], panel_mid[block, :] = split2(values)
    for x, group in enumerate(plan.groups):

        @pl.when((col >> 1) == x)
        def _():
            at = 0
            for cols in group:
                lo = cols[0] * NB
                some = slice(lo, lo + len(cols) * NB)
                product = nt16(
                    jnp.concatenate([panel_high[lo:, :], panel_mid[lo:, :], panel_high[lo:, :]], axis=1),
                    jnp.concatenate([panel_mid[some, :], panel_high[some, :], panel_high[some, :]], axis=1),
                )
                for k, c in enumerate(cols):
                    rows = LAND - c * NB
                    tall[at : at + rows, :] = product[k * NB :, k * NB : (k + 1) * NB]
                    at += rows

    for r in range(plan.pieces):
        start = pl.multiple_of((me ^ r) * plan.piece, 8)
        out, q = (kept_ref, r) if r < plan.pieces // 2 else (sent_ref, r - plan.pieces // 2)
        out[q * plan.piece : (q + 1) * plan.piece, :] = tall[pl.ds(start, plan.piece), :]


def gram_pieces(plan, where, points, halves):
    half = points.shape[0] // 2
    dim = points.shape[1]
    return pl.pallas_call(
        functools.partial(gram_kernel, plan),
        grid_spec=pltpu.PrefetchScalarGridSpec(
            num_scalar_prefetch=1,
            grid=(1,),
            in_specs=[
                pl.BlockSpec((half, dim), lambda i, where: (where[0] & 1, 0)),
            ]
            + [pl.BlockSpec(memory_space=pltpu.VMEM)] * 4,
            out_specs=[pl.BlockSpec(memory_space=pltpu.VMEM)] * 2,
            scratch_shapes=[
                pltpu.VMEM((LAND, dim), F32),
                pltpu.VMEM((LAND, half), BF16),
                pltpu.VMEM((LAND, half), BF16),
                pltpu.VMEM((plan.rows, NB), F32),
            ],
        ),
        out_shape=[jax.ShapeDtypeStruct((plan.rows // 2, NB), F32)] * 2,
        compiler_params=pltpu.CompilerParams(vmem_limit_bytes=36 << 20),
        name="gram",
    )(where, points, *halves)


def lanecast(x, lane):
    index = jnp.full((8, NB), lane, jnp.int32)
    return jnp.take_along_axis(x, index, axis=1, mode="promise_in_bounds")


def rowcast(x, row):
    return jnp.broadcast_to(x[row : row + 1, :], (8, NB))


def eliminate(rows, s, columns, near, lane, sub):
    own, lo = rows[s], 8 * s
    p = list(columns)
    inside = (lane >= lo) & (lane < lo + 8)
    t = [jnp.where(inside, jnp.where(lane == lo + j, 1.0, 0.0), rowcast(own, j)) for j in range(8)]
    last = s + 1 == STRIPS
    if not last:
        c = [lanecast(rows[s + 1], lo + j) for j in range(8)]
        nearest = list(c)
        following = [lanecast(rows[s + 1], lo + 8 + j) for j in range(8)]
    upper, v, scaled = {}, [None] * 8, None
    for j in range(0, 8, 2):
        k = j + 1
        pa, pb, pc = rowcast(p[j], j), rowcast(p[k], j), rowcast(p[k], k)
        det = pa * pc - pb * pb
        inv = 1.0 / det
        gj, gk = inv * (pc * p[j] - pb * p[k]), inv * (pa * p[k] - pb * p[j])
        for l in range(j + 2, 8):
            upper[j, l], upper[k, l] = rowcast(gj, l), rowcast(gk, l)
            p[l] = (p[l] - p[j] * upper[j, l]) - p[k] * upper[k, l]
        if not last:
            gj, gk = inv * (pc * c[j] - pb * c[k]), inv * (pa * c[k] - pb * c[j])
            for l in range(j + 2, 8):
                c[l] = (c[l] - c[j] * upper[j, l]) - c[k] * upper[k, l]
            for l in range(8):
                following[l] = (following[l] - c[j] * rowcast(gj, l)) - c[k] * rowcast(gk, l)
        tw = pa * t[k] - pb * t[j]
        v[j], v[k] = inv * (pc * t[j] - pb * t[k]), inv * tw
        for i in range(j + 2, 8):
            t[i] = (t[i] - upper[j, i] * t[j]) - upper[k, i] * t[k]
        root = lax.rsqrt(pa)
        first, second = t[j] * root, tw * (root * lax.rsqrt(det))
        scaled = first if j == 0 else jnp.where(sub == j, first, scaled)
        scaled = jnp.where(sub == k, second, scaled)
    if last:
        return scaled, None
    for j in range(6, 0, -2):
        for i in range(j):
            v[i] = (v[i] - upper[i, j] * v[j]) - upper[i, j + 1] * v[j + 1]
    for q in range(s + 1, near):
        columns = nearest if q == s + 1 else [lanecast(rows[q], lo + j) for j in range(8)]
        rest = jnp.where(inside, 0.0, rows[q])
        for j in range(7, -1, -1):
            rest = rest - columns[j] * v[j]
        rows[q] = rest
    return scaled, following


GROUP = 4


def factor_inverse(block, inverse):
    lane = lax.broadcasted_iota(jnp.int32, (8, NB), 1)
    sub = lax.broadcasted_iota(jnp.int32, (8, NB), 0)
    rows = [block[8 * q : 8 * q + 8, :] for q in range(STRIPS)]
    columns = [lanecast(rows[0], j) for j in range(8)]
    for g in range(STRIPS // GROUP):
        near = min((g + 2) * GROUP, STRIPS)
        lo, hi = 8 * GROUP * g, 8 * GROUP * (g + 1)
        left, right = [], []
        for s in range(g * GROUP, (g + 1) * GROUP):
            scaled, columns = eliminate(rows, s, columns, near, lane, sub)
            inverse[8 * s : 8 * s + 8, :] = jnp.where(lane < 8 * (s + 1), scaled, 0.0)
            left.append(scaled)
            right.append(jnp.where((lane >= 8 * (s + 1)) & (lane < hi), 0.0, scaled))
        if near < STRIPS:
            left, right = jnp.concatenate(left, axis=0), jnp.concatenate(right, axis=0)
            update = lax.dot_general(
                left[:, 8 * near :], right, (((0,), (0,)), ((), ())), precision=precise, preferred_element_type=F32
            )
            inside = (lane >= lo) & (lane < hi)
            for q in range(near, STRIPS):
                at = 8 * (q - near)
                rows[q] = jnp.where(inside, 0.0, rows[q]) - update[at : at + 8, :]


def cholesky_kernel(plan, where_ref, here0, here1, there0, there1, out_ref, tall, a, block, inv1, inv2, l21):
    col, me = where_ref[0], where_ref[1]
    width = LAND // plan.col
    low = plan.halved - 1
    for rc, rz, pieces_ref in ((0, 0, here0), (0, 1, here1), (1, 0, there0), (1, 1, there1)):
        for r in range(plan.nx << low):
            x = ungray(gray(col >> 1) ^ (r >> low), plan.xbits)
            piece = me ^ ((rc << plan.halved) | (rz << low) | (r & ((1 << low) - 1)))
            start = pl.multiple_of(x * plan.rows + piece * plan.piece, 8)
            tall[pl.ds(start, plan.piece), :] = pieces_ref[r * plan.piece : (r + 1) * plan.piece, :]
    at = 0
    for group in plan.groups:
        for j, c in group_blocks(group):
            a[j * NB : (j + 1) * NB, c * NB : (c + 1) * NB] = tall[at : at + NB, :]
            at += NB

    row = lax.broadcasted_iota(jnp.int32, (NB, NB), 0)
    column = lax.broadcasted_iota(jnp.int32, (NB, NB), 1)

    def step(k, carry):
        base = pl.multiple_of((k // 2) * PAIR, PAIR)
        first = (k % 2) == 0
        for t in range(LAND // PAIR):
            lo = t * PAIR

            @pl.when(k == 2 * t)
            def _():
                if t:
                    update = nt6(a[lo:, :lo], a[lo : lo + PAIR, :lo])
                    a[lo:, lo : lo + PAIR] = a[lo:, lo : lo + PAIR] - update
                block[...] = a[lo : lo + NB, lo : lo + NB]

        @pl.when(jnp.logical_not(first))
        def _():
            below = nt(a[pl.ds(base + NB, NB), pl.ds(base, NB)], inv2[...])
            l21[...] = below
            inv1[...] = inv2[...]
            block[...] = a[pl.ds(base + NB, NB), pl.ds(base + NB, NB)] - nt(below, below)

        factor_inverse(block, inv2)

        for t in range(LAND // PAIR):
            lo = t * PAIR

            @pl.when((k == 2 * t + 1) & (col * width // PAIR == t))
            def _():
                top = slice(lo, lo + NB)
                low = slice(lo + NB, lo + PAIR)
                a[top, top] = jnp.where(column <= row, nt6(a[top, top], inv1[...]), 0.0)
                a[low, top] = l21[...]
                a[low, low] = jnp.where(column <= row, nt6(block[...], inv2[...]), 0.0)

            @pl.when((k == 2 * t + 1) & (lo + PAIR < LAND))
            def _():
                rest = slice(lo + PAIR, LAND)
                if lo + PAIR < LAND:
                    left = nt6(a[rest, lo : lo + NB], inv1[...])
                    right = a[rest, lo + NB : lo + PAIR] - nt6(left, l21[...])
                    a[rest, lo : lo + NB] = left
                    a[rest, lo + NB : lo + PAIR] = nt6(right, inv2[...])

        return carry

    lax.fori_loop(0, BLOCKS, step, 0)

    out_ref[...] = jnp.zeros(out_ref.shape, F32)
    for c in range(plan.col):

        @pl.when(col == c)
        def _():
            for j in range(width // NB):
                at = c * width + j * NB
                for i in range(at // NB + 1):
                    out_ref[i * NB : (i + 1) * NB, j * NB : (j + 1) * NB] = a[at : at + NB, i * NB : (i + 1) * NB].T


def factor(plan, where, parts):
    total = plan.rows * plan.nx
    width = LAND // plan.col
    return pl.pallas_call(
        functools.partial(cholesky_kernel, plan),
        grid_spec=pltpu.PrefetchScalarGridSpec(
            num_scalar_prefetch=1,
            grid=(1,),
            in_specs=[pl.BlockSpec(memory_space=pltpu.VMEM)] * 4,
            out_specs=pl.BlockSpec((LAND, width), lambda i, where: (0, 0)),
            scratch_shapes=[
                pltpu.VMEM((total, NB), F32),
                pltpu.VMEM((LAND, LAND), F32),
                pltpu.VMEM((NB, NB), F32),
                pltpu.VMEM((NB, NB), F32),
                pltpu.VMEM((NB, NB), F32),
                pltpu.VMEM((NB, NB), F32),
            ],
        ),
        out_shape=jax.ShapeDtypeStruct((LAND, width), F32),
        compiler_params=pltpu.CompilerParams(vmem_limit_bytes=28 << 20),
        name="factor",
    )(where, *parts)


def local(points, point_ids, landmark_ids):
    plan = Plan(lax.axis_size("dp"), lax.axis_size("col"))
    col_index, dp_index = lax.axis_index("col"), lax.axis_index("dp")
    where = jnp.stack([col_index, plan.own_piece(col_index, dp_index)]).astype(jnp.int32)

    centers = pick(landmark_ids, point_ids, points)
    halves = jnp.split(centers, 2)
    for k in range(plan.zbits):
        halves = [half + swap(half, "dp", mirror(k)) for half in halves]
    halves = [over_x(plan, half) for half in halves]
    halves = halves + [swap(half, "col", 1) for half in halves]

    kept, sent = gram_pieces(plan, where, points, halves)
    held = kept + swap(sent, "col", 1)
    for k in range(plan.halved):
        half = held.shape[0] // 2
        held = held[:half] + swap(held[half:], "dp", mirror(k))
    for k in range(plan.halved, plan.zbits):
        held = held + swap(held, "dp", mirror(k))
    for k in reversed(range(1, plan.halved)):
        held = jnp.concatenate([held, swap(held, "dp", mirror(k))])
    beside = swap(held, "dp", mirror(0))
    here = [over_x(plan, held), over_x(plan, beside)]
    there = [swap(part, "col", 1) for part in here]
    return factor(plan, where, here + there)


def over_x(plan, part):
    for k in range(plan.xbits):
        part = jnp.concatenate([part, swap(part, "col", 2 * mirror(k))])
    return part


def solution(mesh):
    in_specs = (P(("groups", "dp"), None), P(("groups", "dp")), P(("groups", "col")))
    out_specs = P("groups", "col")
    return jax.shard_map(local, mesh=mesh, in_specs=in_specs, out_specs=out_specs, check_vma=False)
```

```python
import functools

import jax
import jax.numpy as jnp
from jax import lax
from jax.experimental import pallas as pl
from jax.experimental.pallas import tpu as pltpu
from jax.sharding import PartitionSpec as P

LAND = 1024
NB = 128
PAIR = 2 * NB
STRIPS = NB // 8
BLOCKS = LAND // NB
CHUNKS = 2

F32 = jnp.float32
BF16 = jnp.bfloat16
precise = lax.Precision.HIGHEST


def nt(a, b):
    return lax.dot_general(a, b, (((1,), (1,)), ((), ())), precision=precise, preferred_element_type=F32)


def nt16(a, b):
    return lax.dot_general(a, b, (((1,), (1,)), ((), ())), preferred_element_type=F32)


def six(x, other):
    high, mid, low = split3(x)
    return jnp.concatenate([low, mid, high, mid, high, high] if other else [high, mid, low, high, mid, high], axis=1)


def nt6(a, b):
    return nt16(six(a, False), six(b, True))


def split2(x):
    high = x.astype(BF16)
    return high, (x - high.astype(F32)).astype(BF16)


def split3(x):
    high = x.astype(BF16)
    rest = x - high.astype(F32)
    mid = rest.astype(BF16)
    low = (rest - mid.astype(F32)).astype(BF16)
    return high, mid, low


def log2(n):
    bits = n.bit_length() - 1
    assert n == 1 << bits
    return bits


def mirror(k):
    return (2 << k) - 1


def gray(i):
    return i ^ (i >> 1)


def ungray(g, bits):
    i = g
    for s in range(1, bits):
        i = i ^ (g >> s)
    return i


def swap(x, axis, mask):
    n = lax.axis_size(axis)
    return lax.ppermute(x, axis, [(i, i ^ mask) for i in range(n)])


def column_groups(nx):
    if nx == 4:
        return [[(0,), (7,)], [(1,), (6,)], [(2,), (5,)], [(3,), (4,)]]
    assert nx == 2
    return [[(0, 1), (6, 7)], [(2, 3), (4, 5)]]


def group_blocks(group):
    return [(j, c) for cols in group for c in cols for j in range(c, BLOCKS)]


class Plan:
    def __init__(self, dp, col):
        self.dp, self.col = dp, col
        self.nx = col // 2
        self.xbits, self.zbits = log2(self.nx), log2(dp)
        self.groups = column_groups(self.nx)
        self.rows = len(group_blocks(self.groups[0])) * NB
        rows = self.rows // CHUNKS // 2
        self.halved = 0
        while self.halved < max(1, self.zbits - 1) and rows % 16 == 0:
            rows //= 2
            self.halved += 1
        self.piece = rows
        self.pieces = 2 << self.halved

    def own_piece(self, col_index, dp_index):
        g = gray(dp_index)
        s = col_index & 1
        for k in range(self.halved):
            s = (s << 1) | ((g >> k) & 1)
        return s


def pick_kernel(lid_ref, pid_ref, points_ref, out_ref):
    n = lid_ref.shape[1]
    goes_first = (gray(lax.axis_index("dp")) & 1) == 1
    ids = jnp.broadcast_to(lid_ref[...].astype(F32), (8, n))
    ids = jnp.where(goes_first, pltpu.roll(ids, n // 2, 1), ids)
    matches = jnp.where(ids.T[:, 0:1] == pid_ref[...].astype(F32), 1.0, 0.0).astype(BF16)
    high, mid, low = split3(points_ref[...])
    dot = functools.partial(jnp.dot, preferred_element_type=F32)
    out_ref[...] = (dot(matches, high) + dot(matches, mid)) + dot(matches, low)


def pick(landmark_ids, point_ids, points):
    n = landmark_ids.shape[0]
    return pl.pallas_call(
        pick_kernel,
        out_shape=jax.ShapeDtypeStruct((n, points.shape[1]), F32),
        out_specs=pl.BlockSpec(memory_space=pltpu.VMEM),
        compiler_params=pltpu.CompilerParams(vmem_limit_bytes=36 << 20),
        name="pick",
    )(landmark_ids.reshape(1, n), point_ids.reshape(1, -1), points)


def gram_kernel(plan, where_ref, points_ref, *refs):
    parts, refs = refs[:4], refs[4:]
    outs = refs[: 2 * CHUNKS]
    centers, panel_high, panel_mid, tall = refs[2 * CHUNKS :]
    col, me, first = where_ref[0], where_ref[1], where_ref[2]
    some = LAND // plan.col // 2
    dim = points_ref.shape[1]
    for n, centers_ref in enumerate(parts):
        rc, rz = n // 2, n % 2
        for rx in range(plan.nx):
            x = ungray(gray(col >> 1) ^ rx, plan.xbits)
            owner = (x << 1) | ((col & 1) ^ rc)
            at = pl.multiple_of((owner * 2 + (first ^ rz)) * some, some)
            centers[pl.ds(at, some), :] = centers_ref[rx * some : (rx + 1) * some, :]
    pts = points_ref[...]
    point_norms = nt(jnp.ones((8, dim), F32), pts * pts)[0:1, :]
    right = six(pts, True)
    for b in range(LAND // PAIR):
        block = slice(b * PAIR, (b + 1) * PAIR)
        c = centers[block, :]
        center_norms = jnp.sum(c * c, axis=1, keepdims=True)
        inner = nt16(six(c, False), right)
        distance = point_norms + center_norms - 2.0 * inner
        values = jnp.exp(distance * (-2.0 / dim))
        panel_high[block, :], panel_mid[block, :] = split2(values)
    for x, group in enumerate(plan.groups):

        @pl.when((col >> 1) == x)
        def _():
            at = 0
            for cols in group:
                lo = cols[0] * NB
                some = slice(lo, lo + len(cols) * NB)
                product = nt16(
                    jnp.concatenate([panel_high[lo:, :], panel_mid[lo:, :], panel_high[lo:, :]], axis=1),
                    jnp.concatenate([panel_mid[some, :], panel_high[some, :], panel_high[some, :]], axis=1),
                )
                for k, c in enumerate(cols):
                    rows = LAND - c * NB
                    tall[at : at + rows, :] = product[k * NB :, k * NB : (k + 1) * NB]
                    at += rows

    for chunk in range(CHUNKS):
        for r in range(plan.pieces):
            start = pl.multiple_of((chunk * plan.pieces + (me ^ r)) * plan.piece, 8)
            side, q = divmod(r, plan.pieces // 2)
            outs[2 * chunk + side][q * plan.piece : (q + 1) * plan.piece, :] = tall[pl.ds(start, plan.piece), :]


def gram_pieces(plan, where, points, parts):
    half = points.shape[0] // 2
    dim = points.shape[1]
    return pl.pallas_call(
        functools.partial(gram_kernel, plan),
        grid_spec=pltpu.PrefetchScalarGridSpec(
            num_scalar_prefetch=1,
            grid=(1,),
            in_specs=[
                pl.BlockSpec((half, dim), lambda i, where: (where[0] & 1, 0)),
            ]
            + [pl.BlockSpec(memory_space=pltpu.VMEM)] * 4,
            out_specs=[pl.BlockSpec(memory_space=pltpu.VMEM)] * (2 * CHUNKS),
            scratch_shapes=[
                pltpu.VMEM((LAND, dim), F32),
                pltpu.VMEM((LAND, half), BF16),
                pltpu.VMEM((LAND, half), BF16),
                pltpu.VMEM((plan.rows, NB), F32),
            ],
        ),
        out_shape=[jax.ShapeDtypeStruct((plan.rows // (2 * CHUNKS), NB), F32)] * (2 * CHUNKS),
        compiler_params=pltpu.CompilerParams(vmem_limit_bytes=36 << 20),
        name="gram",
    )(where, points, *parts)


def lanecast(x, lane):
    index = jnp.full((8, NB), lane, jnp.int32)
    return jnp.take_along_axis(x, index, axis=1, mode="promise_in_bounds")


def rowcast(x, row):
    return jnp.broadcast_to(x[row : row + 1, :], (8, NB))


def eliminate(rows, s, columns, near, lane, sub):
    own, lo = rows[s], 8 * s
    p = list(columns)
    inside = (lane >= lo) & (lane < lo + 8)
    t = [jnp.where(inside, jnp.where(lane == lo + j, 1.0, 0.0), rowcast(own, j)) for j in range(8)]
    last = s + 1 == STRIPS
    if not last:
        c = [lanecast(rows[s + 1], lo + j) for j in range(8)]
        nearest = list(c)
        following = [lanecast(rows[s + 1], lo + 8 + j) for j in range(8)]
    upper, v, scaled = {}, [None] * 8, None
    for j in range(0, 8, 2):
        k = j + 1
        pa, pb, pc = rowcast(p[j], j), rowcast(p[k], j), rowcast(p[k], k)
        det = pa * pc - pb * pb
        inv = 1.0 / det
        gj, gk = inv * (pc * p[j] - pb * p[k]), inv * (pa * p[k] - pb * p[j])
        for l in range(j + 2, 8):
            upper[j, l], upper[k, l] = rowcast(gj, l), rowcast(gk, l)
            p[l] = (p[l] - p[j] * upper[j, l]) - p[k] * upper[k, l]
        if not last:
            gj, gk = inv * (pc * c[j] - pb * c[k]), inv * (pa * c[k] - pb * c[j])
            for l in range(j + 2, 8):
                c[l] = (c[l] - c[j] * upper[j, l]) - c[k] * upper[k, l]
            for l in range(8):
                following[l] = (following[l] - c[j] * rowcast(gj, l)) - c[k] * rowcast(gk, l)
        tw = pa * t[k] - pb * t[j]
        v[j], v[k] = inv * (pc * t[j] - pb * t[k]), inv * tw
        for i in range(j + 2, 8):
            t[i] = (t[i] - upper[j, i] * t[j]) - upper[k, i] * t[k]
        root = lax.rsqrt(pa)
        first, second = t[j] * root, tw * (root * lax.rsqrt(det))
        scaled = first if j == 0 else jnp.where(sub == j, first, scaled)
        scaled = jnp.where(sub == k, second, scaled)
    if last:
        return scaled, None
    for j in range(6, 0, -2):
        for i in range(j):
            v[i] = (v[i] - upper[i, j] * v[j]) - upper[i, j + 1] * v[j + 1]
    for q in range(s + 1, near):
        columns = nearest if q == s + 1 else [lanecast(rows[q], lo + j) for j in range(8)]
        rest = jnp.where(inside, 0.0, rows[q])
        for j in range(7, -1, -1):
            rest = rest - columns[j] * v[j]
        rows[q] = rest
    return scaled, following


GROUP = 4


def factor_inverse(block, inverse):
    lane = lax.broadcasted_iota(jnp.int32, (8, NB), 1)
    sub = lax.broadcasted_iota(jnp.int32, (8, NB), 0)
    rows = [block[8 * q : 8 * q + 8, :] for q in range(STRIPS)]
    columns = [lanecast(rows[0], j) for j in range(8)]
    for g in range(STRIPS // GROUP):
        near = min((g + 2) * GROUP, STRIPS)
        lo, hi = 8 * GROUP * g, 8 * GROUP * (g + 1)
        left, right = [], []
        for s in range(g * GROUP, (g + 1) * GROUP):
            scaled, columns = eliminate(rows, s, columns, near, lane, sub)
            inverse[8 * s : 8 * s + 8, :] = jnp.where(lane < 8 * (s + 1), scaled, 0.0)
            left.append(scaled)
            right.append(jnp.where((lane >= 8 * (s + 1)) & (lane < hi), 0.0, scaled))
        if near < STRIPS:
            left, right = jnp.concatenate(left, axis=0), jnp.concatenate(right, axis=0)
            update = lax.dot_general(
                left[:, 8 * near :], right, (((0,), (0,)), ((), ())), precision=precise, preferred_element_type=F32
            )
            inside = (lane >= lo) & (lane < hi)
            for q in range(near, STRIPS):
                at = 8 * (q - near)
                rows[q] = jnp.where(inside, 0.0, rows[q]) - update[at : at + 8, :]


def cholesky_kernel(plan, where_ref, *refs):
    parts = refs[: 4 * CHUNKS]
    out_ref, tall, a, block, inv1, inv2, l21 = refs[4 * CHUNKS :]
    col, me = where_ref[0], where_ref[1]
    width = LAND // plan.col
    low = plan.halved - 1
    for n, pieces_ref in enumerate(parts):
        rc, chunk, rz = n // (2 * CHUNKS), n // 2 % CHUNKS, n % 2
        for r in range(plan.nx << low):
            x = ungray(gray(col >> 1) ^ (r >> low), plan.xbits)
            piece = me ^ ((rc << plan.halved) | (rz << low) | (r & ((1 << low) - 1)))
            start = pl.multiple_of(x * plan.rows + (chunk * plan.pieces + piece) * plan.piece, 8)
            tall[pl.ds(start, plan.piece), :] = pieces_ref[r * plan.piece : (r + 1) * plan.piece, :]
    at = 0
    for group in plan.groups:
        for j, c in group_blocks(group):
            a[j * NB : (j + 1) * NB, c * NB : (c + 1) * NB] = tall[at : at + NB, :]
            at += NB

    row = lax.broadcasted_iota(jnp.int32, (NB, NB), 0)
    column = lax.broadcasted_iota(jnp.int32, (NB, NB), 1)

    def step(k, carry):
        base = pl.multiple_of((k // 2) * PAIR, PAIR)
        first = (k % 2) == 0
        for t in range(LAND // PAIR):
            lo = t * PAIR

            @pl.when(k == 2 * t)
            def _():
                if t:
                    update = nt6(a[lo:, :lo], a[lo : lo + PAIR, :lo])
                    a[lo:, lo : lo + PAIR] = a[lo:, lo : lo + PAIR] - update
                block[...] = a[lo : lo + NB, lo : lo + NB]

        @pl.when(jnp.logical_not(first))
        def _():
            below = nt(a[pl.ds(base + NB, NB), pl.ds(base, NB)], inv2[...])
            l21[...] = below
            inv1[...] = inv2[...]
            block[...] = a[pl.ds(base + NB, NB), pl.ds(base + NB, NB)] - nt(below, below)

        factor_inverse(block, inv2)

        for t in range(LAND // PAIR):
            lo = t * PAIR

            @pl.when((k == 2 * t + 1) & (col * width // PAIR == t))
            def _():
                top = slice(lo, lo + NB)
                low = slice(lo + NB, lo + PAIR)
                a[top, top] = jnp.where(column <= row, nt6(a[top, top], inv1[...]), 0.0)
                a[low, top] = l21[...]
                a[low, low] = jnp.where(column <= row, nt6(block[...], inv2[...]), 0.0)

            @pl.when((k == 2 * t + 1) & (lo + PAIR < LAND))
            def _():
                rest = slice(lo + PAIR, LAND)
                if lo + PAIR < LAND:
                    left = nt6(a[rest, lo : lo + NB], inv1[...])
                    right = a[rest, lo + NB : lo + PAIR] - nt6(left, l21[...])
                    a[rest, lo : lo + NB] = left
                    a[rest, lo + NB : lo + PAIR] = nt6(right, inv2[...])

        return carry

    lax.fori_loop(0, BLOCKS, step, 0)

    out_ref[...] = jnp.zeros(out_ref.shape, F32)
    for c in range(plan.col):

        @pl.when(col == c)
        def _():
            for j in range(width // NB):
                at = c * width + j * NB
                for i in range(at // NB + 1):
                    out_ref[i * NB : (i + 1) * NB, j * NB : (j + 1) * NB] = a[at : at + NB, i * NB : (i + 1) * NB].T


def factor(plan, where, parts):
    total = plan.rows * plan.nx
    width = LAND // plan.col
    return pl.pallas_call(
        functools.partial(cholesky_kernel, plan),
        grid_spec=pltpu.PrefetchScalarGridSpec(
            num_scalar_prefetch=1,
            grid=(1,),
            in_specs=[pl.BlockSpec(memory_space=pltpu.VMEM)] * (4 * CHUNKS),
            out_specs=pl.BlockSpec((LAND, width), lambda i, where: (0, 0)),
            scratch_shapes=[
                pltpu.VMEM((total, NB), F32),
                pltpu.VMEM((LAND, LAND), F32),
                pltpu.VMEM((NB, NB), F32),
                pltpu.VMEM((NB, NB), F32),
                pltpu.VMEM((NB, NB), F32),
                pltpu.VMEM((NB, NB), F32),
            ],
        ),
        out_shape=jax.ShapeDtypeStruct((LAND, width), F32),
        compiler_params=pltpu.CompilerParams(vmem_limit_bytes=28 << 20),
        name="factor",
    )(where, *parts)


def local(points, point_ids, landmark_ids):
    plan = Plan(lax.axis_size("dp"), lax.axis_size("col"))
    col_index, dp_index = lax.axis_index("col"), lax.axis_index("dp")
    bit = gray(dp_index) & 1
    where = jnp.stack([col_index, plan.own_piece(col_index, dp_index), bit]).astype(jnp.int32)

    held = [half_over_dp(pick(landmark_ids, point_ids, points), 0)]
    for k in range(1, plan.zbits):
        held = [part + swap(part, "dp", mirror(k)) for part in held]
    here = [over_x(plan, side) for part in held for side in (part, swap(part, "dp", mirror(0)))]
    there = [swap(part, "col", 1) for part in here]

    sums = gram_pieces(plan, where, points, here + there)
    held = [kept + swap(sent, "col", 1) for kept, sent in zip(sums[::2], sums[1::2])]
    for k in range(plan.halved):
        held = [half_over_dp(part, k) for part in held]
    for k in range(plan.halved, plan.zbits):
        held = [part + swap(part, "dp", mirror(k)) for part in held]
    for k in reversed(range(1, plan.halved)):
        held = [jnp.concatenate([part, swap(part, "dp", mirror(k))]) for part in held]
    here = [over_x(plan, side) for part in held for side in (part, swap(part, "dp", mirror(0)))]
    there = [swap(part, "col", 1) for part in here]
    return factor(plan, where, here + there)


def half_over_dp(part, k):
    half = part.shape[0] // 2
    return part[:half] + swap(part[half:], "dp", mirror(k))


def over_x(plan, part):
    for k in range(plan.xbits):
        part = jnp.concatenate([part, swap(part, "col", 2 * mirror(k))])
    return part


def solution(mesh):
    in_specs = (P(("groups", "dp"), None), P(("groups", "dp")), P(("groups", "col")))
    out_specs = P("groups", "col")
    return jax.shard_map(local, mesh=mesh, in_specs=in_specs, out_specs=out_specs, check_vma=False)
```

```python
import functools

import jax
import jax.numpy as jnp
from jax import lax
from jax.experimental import pallas as pl
from jax.experimental.pallas import tpu as pltpu
from jax.sharding import PartitionSpec as P

LAND = 1024
NB = 128
PAIR = 2 * NB
STRIPS = NB // 8
BLOCKS = LAND // NB
CHUNKS = 2

F32 = jnp.float32
BF16 = jnp.bfloat16
precise = lax.Precision.HIGHEST


def nt(a, b):
    return lax.dot_general(a, b, (((1,), (1,)), ((), ())), precision=precise, preferred_element_type=F32)


def nt16(a, b):
    return lax.dot_general(a, b, (((1,), (1,)), ((), ())), preferred_element_type=F32)


def six(x, other):
    high, mid, low = split3(x)
    return jnp.concatenate([low, mid, high, mid, high, high] if other else [high, mid, low, high, mid, high], axis=1)


def nt6(a, b):
    return nt16(six(a, False), six(b, True))


def split2(x):
    high = x.astype(BF16)
    return high, (x - high.astype(F32)).astype(BF16)


def split3(x):
    high = x.astype(BF16)
    rest = x - high.astype(F32)
    mid = rest.astype(BF16)
    low = (rest - mid.astype(F32)).astype(BF16)
    return high, mid, low


def log2(n):
    bits = n.bit_length() - 1
    assert n == 1 << bits
    return bits


def mirror(k):
    return (2 << k) - 1


def gray(i):
    return i ^ (i >> 1)


def ungray(g, bits):
    i = g
    for s in range(1, bits):
        i = i ^ (g >> s)
    return i


def swap(x, axis, mask):
    n = lax.axis_size(axis)
    return lax.ppermute(x, axis, [(i, i ^ mask) for i in range(n)])


def column_groups(nx):
    if nx == 4:
        return [[(0,), (7,)], [(1,), (6,)], [(2,), (5,)], [(3,), (4,)]]
    assert nx == 2
    return [[(0, 1), (6, 7)], [(2, 3), (4, 5)]]


def group_blocks(group):
    return [(j, c) for cols in group for c in cols for j in range(c, BLOCKS)]


class Plan:
    def __init__(self, dp, col):
        self.dp, self.col = dp, col
        self.nx = col // 2
        self.xbits, self.zbits = log2(self.nx), log2(dp)
        self.groups = column_groups(self.nx)
        self.rows = len(group_blocks(self.groups[0])) * NB
        rows = self.rows // CHUNKS // 2
        self.halved = 0
        while self.halved < max(1, self.zbits - 1) and rows % 16 == 0:
            rows //= 2
            self.halved += 1
        self.piece = rows
        self.pieces = 2 << self.halved

    def own_piece(self, col_index, dp_index):
        g = gray(dp_index)
        s = col_index & 1
        for k in range(self.halved):
            s = (s << 1) | ((g >> k) & 1)
        return s


def pick_kernel(lid_ref, pid_ref, points_ref, out_ref):
    n = lid_ref.shape[1]
    goes_first = (gray(lax.axis_index("dp")) & 1) == 1
    ids = jnp.broadcast_to(lid_ref[...].astype(F32), (8, n))
    ids = jnp.where(goes_first, pltpu.roll(ids, n // 2, 1), ids)
    matches = jnp.where(ids.T[:, 0:1] == pid_ref[...].astype(F32), 1.0, 0.0).astype(BF16)
    high, mid, low = split3(points_ref[...])
    dot = functools.partial(jnp.dot, preferred_element_type=F32)
    out_ref[...] = (dot(matches, high) + dot(matches, mid)) + dot(matches, low)


def pick(landmark_ids, point_ids, points):
    n = landmark_ids.shape[0]
    return pl.pallas_call(
        pick_kernel,
        out_shape=jax.ShapeDtypeStruct((n, points.shape[1]), F32),
        out_specs=pl.BlockSpec(memory_space=pltpu.VMEM),
        compiler_params=pltpu.CompilerParams(vmem_limit_bytes=36 << 20),
        name="pick",
    )(landmark_ids.reshape(1, n), point_ids.reshape(1, -1), points)


def gram_kernel(plan, where_ref, points_ref, *refs):
    parts, refs = refs[:4], refs[4:]
    outs = refs[: 2 * CHUNKS]
    centers, panel_high, panel_mid, tall = refs[2 * CHUNKS :]
    col, me, first = where_ref[0], where_ref[1], where_ref[2]
    some = LAND // plan.col // 2
    dim = points_ref.shape[1]
    for n, centers_ref in enumerate(parts):
        rc, rz = n // 2, n % 2
        for rx in range(plan.nx):
            x = ungray(gray(col >> 1) ^ rx, plan.xbits)
            owner = (x << 1) | ((col & 1) ^ rc)
            at = pl.multiple_of((owner * 2 + (first ^ rz)) * some, some)
            centers[pl.ds(at, some), :] = centers_ref[rx * some : (rx + 1) * some, :]
    pts = points_ref[...]
    point_norms = nt(jnp.ones((8, dim), F32), pts * pts)[0:1, :]
    right = six(pts, True)
    for b in range(LAND // PAIR):
        block = slice(b * PAIR, (b + 1) * PAIR)
        c = centers[block, :]
        center_norms = jnp.sum(c * c, axis=1, keepdims=True)
        inner = nt16(six(c, False), right)
        distance = point_norms + center_norms - 2.0 * inner
        values = jnp.exp(distance * (-2.0 / dim))
        panel_high[block, :], panel_mid[block, :] = split2(values)
    for x, group in enumerate(plan.groups):

        @pl.when((col >> 1) == x)
        def _():
            at = 0
            for cols in group:
                lo = cols[0] * NB
                some = slice(lo, lo + len(cols) * NB)
                product = nt16(
                    jnp.concatenate([panel_high[lo:, :], panel_mid[lo:, :], panel_high[lo:, :]], axis=1),
                    jnp.concatenate([panel_mid[some, :], panel_high[some, :], panel_high[some, :]], axis=1),
                )
                for k, c in enumerate(cols):
                    rows = LAND - c * NB
                    tall[at : at + rows, :] = product[k * NB :, k * NB : (k + 1) * NB]
                    at += rows

    for chunk in range(CHUNKS):
        for r in range(plan.pieces):
            start = pl.multiple_of((chunk * plan.pieces + (me ^ r)) * plan.piece, 8)
            side, q = divmod(r, plan.pieces // 2)
            outs[2 * chunk + side][q * plan.piece : (q + 1) * plan.piece, :] = tall[pl.ds(start, plan.piece), :]


def gram_pieces(plan, where, points, parts):
    half = points.shape[0] // 2
    dim = points.shape[1]
    return pl.pallas_call(
        functools.partial(gram_kernel, plan),
        grid_spec=pltpu.PrefetchScalarGridSpec(
            num_scalar_prefetch=1,
            grid=(1,),
            in_specs=[
                pl.BlockSpec((half, dim), lambda i, where: (where[0] & 1, 0)),
            ]
            + [pl.BlockSpec(memory_space=pltpu.VMEM)] * 4,
            out_specs=[pl.BlockSpec(memory_space=pltpu.VMEM)] * (2 * CHUNKS),
            scratch_shapes=[
                pltpu.VMEM((LAND, dim), F32),
                pltpu.VMEM((LAND, half), BF16),
                pltpu.VMEM((LAND, half), BF16),
                pltpu.VMEM((plan.rows, NB), F32),
            ],
        ),
        out_shape=[jax.ShapeDtypeStruct((plan.rows // (2 * CHUNKS), NB), F32)] * (2 * CHUNKS),
        compiler_params=pltpu.CompilerParams(vmem_limit_bytes=36 << 20),
        name="gram",
    )(where, points, *parts)


def lanecast(x, lane):
    index = jnp.full((8, NB), lane, jnp.int32)
    return jnp.take_along_axis(x, index, axis=1, mode="promise_in_bounds")


def rowcast(x, row):
    return jnp.broadcast_to(x[row : row + 1, :], (8, NB))


def eliminate(rows, s, columns, near, lane, sub):
    own, lo = rows[s], 8 * s
    p = list(columns)
    inside = (lane >= lo) & (lane < lo + 8)
    t = [jnp.where(inside, jnp.where(lane == lo + j, 1.0, 0.0), rowcast(own, j)) for j in range(8)]
    last = s + 1 == STRIPS
    if not last:
        c = [lanecast(rows[s + 1], lo + j) for j in range(8)]
        nearest = list(c)
        following = [lanecast(rows[s + 1], lo + 8 + j) for j in range(8)]
    upper, v, scaled = {}, [None] * 8, None
    for j in range(0, 8, 2):
        k = j + 1
        pa, pb, pc = rowcast(p[j], j), rowcast(p[k], j), rowcast(p[k], k)
        det = pa * pc - pb * pb
        inv = 1.0 / det
        gj, gk = inv * (pc * p[j] - pb * p[k]), inv * (pa * p[k] - pb * p[j])
        for l in range(j + 2, 8):
            upper[j, l], upper[k, l] = rowcast(gj, l), rowcast(gk, l)
            p[l] = (p[l] - p[j] * upper[j, l]) - p[k] * upper[k, l]
        if not last:
            gj, gk = inv * (pc * c[j] - pb * c[k]), inv * (pa * c[k] - pb * c[j])
            for l in range(j + 2, 8):
                c[l] = (c[l] - c[j] * upper[j, l]) - c[k] * upper[k, l]
            for l in range(8):
                following[l] = (following[l] - c[j] * rowcast(gj, l)) - c[k] * rowcast(gk, l)
        tw = pa * t[k] - pb * t[j]
        v[j], v[k] = inv * (pc * t[j] - pb * t[k]), inv * tw
        for i in range(j + 2, 8):
            t[i] = (t[i] - upper[j, i] * t[j]) - upper[k, i] * t[k]
        root = lax.rsqrt(pa)
        first, second = t[j] * root, tw * (root * lax.rsqrt(det))
        scaled = first if j == 0 else jnp.where(sub == j, first, scaled)
        scaled = jnp.where(sub == k, second, scaled)
    if last:
        return scaled, None
    for j in range(6, 0, -2):
        for i in range(j):
            v[i] = (v[i] - upper[i, j] * v[j]) - upper[i, j + 1] * v[j + 1]
    for q in range(s + 1, near):
        columns = nearest if q == s + 1 else [lanecast(rows[q], lo + j) for j in range(8)]
        rest = jnp.where(inside, 0.0, rows[q])
        for j in range(7, -1, -1):
            rest = rest - columns[j] * v[j]
        rows[q] = rest
    return scaled, following


GROUP = 4


def factor_inverse(block, inverse):
    lane = lax.broadcasted_iota(jnp.int32, (8, NB), 1)
    sub = lax.broadcasted_iota(jnp.int32, (8, NB), 0)
    rows = [block[8 * q : 8 * q + 8, :] for q in range(STRIPS)]
    columns = [lanecast(rows[0], j) for j in range(8)]
    for g in range(STRIPS // GROUP):
        near = min((g + 2) * GROUP, STRIPS)
        lo, hi = 8 * GROUP * g, 8 * GROUP * (g + 1)
        left, right = [], []
        for s in range(g * GROUP, (g + 1) * GROUP):
            scaled, columns = eliminate(rows, s, columns, near, lane, sub)
            inverse[8 * s : 8 * s + 8, :] = jnp.where(lane < 8 * (s + 1), scaled, 0.0)
            left.append(scaled)
            right.append(jnp.where((lane >= 8 * (s + 1)) & (lane < hi), 0.0, scaled))
        if near < STRIPS:
            left, right = jnp.concatenate(left, axis=0), jnp.concatenate(right, axis=0)
            update = lax.dot_general(
                left[:, 8 * near :], right, (((0,), (0,)), ((), ())), precision=precise, preferred_element_type=F32
            )
            inside = (lane >= lo) & (lane < hi)
            for q in range(near, STRIPS):
                at = 8 * (q - near)
                rows[q] = jnp.where(inside, 0.0, rows[q]) - update[at : at + 8, :]


def cholesky_kernel(plan, where_ref, *refs):
    parts = refs[: 4 * CHUNKS]
    out_ref, tall, a, block, inv1, inv2, l21 = refs[4 * CHUNKS :]
    col, me = where_ref[0], where_ref[1]
    width = LAND // plan.col
    low = plan.halved - 1
    for n, pieces_ref in enumerate(parts):
        rc, chunk, rz = n // (2 * CHUNKS), n // 2 % CHUNKS, n % 2
        for r in range(plan.nx << low):
            x = ungray(gray(col >> 1) ^ (r >> low), plan.xbits)
            piece = me ^ ((rc << plan.halved) | (rz << low) | (r & ((1 << low) - 1)))
            start = pl.multiple_of(x * plan.rows + (chunk * plan.pieces + piece) * plan.piece, 8)
            tall[pl.ds(start, plan.piece), :] = pieces_ref[r * plan.piece : (r + 1) * plan.piece, :]
    at = 0
    for group in plan.groups:
        for j, c in group_blocks(group):
            a[j * NB : (j + 1) * NB, c * NB : (c + 1) * NB] = tall[at : at + NB, :]
            at += NB

    row = lax.broadcasted_iota(jnp.int32, (NB, NB), 0)
    column = lax.broadcasted_iota(jnp.int32, (NB, NB), 1)

    def step(k, carry):
        base = pl.multiple_of((k // 2) * PAIR, PAIR)
        first = (k % 2) == 0
        for t in range(LAND // PAIR):
            lo = t * PAIR

            @pl.when(k == 2 * t)
            def _():
                if t:
                    update = nt6(a[lo:, :lo], a[lo : lo + PAIR, :lo])
                    a[lo:, lo : lo + PAIR] = a[lo:, lo : lo + PAIR] - update
                block[...] = a[lo : lo + NB, lo : lo + NB]

        @pl.when(jnp.logical_not(first))
        def _():
            below = nt6(a[pl.ds(base + NB, NB), pl.ds(base, NB)], inv2[...])
            l21[...] = below
            inv1[...] = inv2[...]
            block[...] = a[pl.ds(base + NB, NB), pl.ds(base + NB, NB)] - nt6(below, below)

        factor_inverse(block, inv2)

        for t in range(LAND // PAIR):
            lo = t * PAIR

            @pl.when((k == 2 * t + 1) & (col * width // PAIR == t))
            def _():
                top = slice(lo, lo + NB)
                low = slice(lo + NB, lo + PAIR)
                a[top, top] = jnp.where(column <= row, nt6(a[top, top], inv1[...]), 0.0)
                a[low, top] = l21[...]
                a[low, low] = jnp.where(column <= row, nt6(block[...], inv2[...]), 0.0)

            @pl.when((k == 2 * t + 1) & (lo + PAIR < LAND))
            def _():
                rest = slice(lo + PAIR, LAND)
                if lo + PAIR < LAND:
                    left = nt6(a[rest, lo : lo + NB], inv1[...])
                    right = a[rest, lo + NB : lo + PAIR] - nt6(left, l21[...])
                    a[rest, lo : lo + NB] = left
                    a[rest, lo + NB : lo + PAIR] = nt6(right, inv2[...])

        return carry

    lax.fori_loop(0, BLOCKS, step, 0)

    for c in range(plan.col):

        @pl.when(col == c)
        def _():
            for j in range(width // NB):
                at = c * width + j * NB
                for i in range(at // NB + 1, BLOCKS):
                    out_ref[i * NB : (i + 1) * NB, j * NB : (j + 1) * NB] = jnp.zeros((NB, NB), F32)
                for i in range(at // NB + 1):
                    out_ref[i * NB : (i + 1) * NB, j * NB : (j + 1) * NB] = a[at : at + NB, i * NB : (i + 1) * NB].T


def factor(plan, where, parts):
    total = plan.rows * plan.nx
    width = LAND // plan.col
    return pl.pallas_call(
        functools.partial(cholesky_kernel, plan),
        grid_spec=pltpu.PrefetchScalarGridSpec(
            num_scalar_prefetch=1,
            grid=(1,),
            in_specs=[pl.BlockSpec(memory_space=pltpu.VMEM)] * (4 * CHUNKS),
            out_specs=pl.BlockSpec((LAND, width), lambda i, where: (0, 0)),
            scratch_shapes=[
                pltpu.VMEM((total, NB), F32),
                pltpu.VMEM((LAND, LAND), F32),
                pltpu.VMEM((NB, NB), F32),
                pltpu.VMEM((NB, NB), F32),
                pltpu.VMEM((NB, NB), F32),
                pltpu.VMEM((NB, NB), F32),
            ],
        ),
        out_shape=jax.ShapeDtypeStruct((LAND, width), F32),
        compiler_params=pltpu.CompilerParams(vmem_limit_bytes=28 << 20),
        name="factor",
    )(where, *parts)


def local(points, point_ids, landmark_ids):
    plan = Plan(lax.axis_size("dp"), lax.axis_size("col"))
    col_index, dp_index = lax.axis_index("col"), lax.axis_index("dp")
    bit = gray(dp_index) & 1
    where = jnp.stack([col_index, plan.own_piece(col_index, dp_index), bit]).astype(jnp.int32)

    held = [half_over_dp(pick(landmark_ids, point_ids, points), 0)]
    for k in range(1, plan.zbits):
        held = [part + swap(part, "dp", mirror(k)) for part in held]
    here = [over_x(plan, side) for part in held for side in (part, swap(part, "dp", mirror(0)))]
    there = [swap(part, "col", 1) for part in here]

    sums = gram_pieces(plan, where, points, here + there)
    held = [kept + swap(sent, "col", 1) for kept, sent in zip(sums[::2], sums[1::2])]
    for k in range(plan.halved):
        held = [half_over_dp(part, k) for part in held]
    for k in range(plan.halved, plan.zbits):
        held = [part + swap(part, "dp", mirror(k)) for part in held]
    for k in reversed(range(1, plan.halved)):
        held = [jnp.concatenate([part, swap(part, "dp", mirror(k))]) for part in held]
    here = [over_x(plan, side) for part in held for side in (part, swap(part, "dp", mirror(0)))]
    there = [swap(part, "col", 1) for part in here]
    return factor(plan, where, here + there)


def half_over_dp(part, k):
    half = part.shape[0] // 2
    return part[:half] + swap(part[half:], "dp", mirror(k))


def over_x(plan, part):
    for k in range(plan.xbits):
        part = jnp.concatenate([part, swap(part, "col", 2 * mirror(k))])
    return part


def solution(mesh):
    in_specs = (P(("groups", "dp"), None), P(("groups", "dp")), P(("groups", "col")))
    out_specs = P("groups", "col")
    return jax.shard_map(local, mesh=mesh, in_specs=in_specs, out_specs=out_specs, check_vma=False)
```
